32 devices in a mesh: seq: 8 (over y, x, core), fsdp: 4 (over z).
Axes of the slice: x: 2, y: 2, z: 4, core: 2. Of those that a mesh axis runs over, the one named last changes fastest.
Arguments:
- queries: bfloat16 [4, 2048, 4096], P('fsdp', 'seq'), may hold values from -1000 to 1000
- keys: bfloat16 [4, 2048, 4096], P('fsdp', 'seq'), may hold values from -1000 to 1000
- values: bfloat16 [4, 2048, 4096], P('fsdp', 'seq'), may hold values from -24 to 24
- targets: bfloat16 [4, 2048, 4096], P('fsdp', 'seq'), may hold values from -2.390625 to 2.390625
- tile_lists: int32 [4, 128, 12], P('fsdp', 'seq'), may hold values from 0 to 127, as said below
- query_gain: float32 [4096], P('fsdp'), may hold values from 0.1 to 1.9
- key_gain: float32 [4096], P('fsdp'), may hold values from 0.1 to 1.9
Outputs:
- grad_queries: bfloat16 [4, 2048, 4096], P('fsdp', 'seq')
- grad_keys: bfloat16 [4, 2048, 4096], P('fsdp', 'seq')
- grad_values: bfloat16 [4, 2048, 4096], P('fsdp', 'seq')
- grad_query_gain: float32 [4096], P('fsdp')
- grad_key_gain: float32 [4096], P('fsdp')
The draws below stay inside these ranges and needn't reach their ends.
Inputs may be any that keep to these rules, and one draw needn't show every extreme that they name: `tile_lists`: tiles are numbered frame by frame and, inside a frame of 4 by 4 tiles, row by row. Entry 0 of each list is the query tile itself; every entry names a tile at most one frame, one tile row and one tile column away from the query tile; entries may repeat.
All inputs are finite; a program needn't handle non-finite values.
Results may differ from the reference program's by a relative error of at most 0.022.
The reference program's roundings to bfloat16 on the way count: a program that leaves them out, or rounds other values in their place, can miss the bound.
Values may be sent and summed in bfloat16 or wider, within the bound.
A program may use at most 192 MiB of HBM per device.

```python
import math
import jax
import jax.numpy as jnp
from jax import lax

HEADS = 32
HD = 128
TILE = 16
GRID_W = 4
GRID_H = 4
KT = 12
QKV = 4096
TPF = 16
FT = 256
FRAMES = 8
SEQ = 2048
SAMPLES = 4


def field_draw(key, stream):
    field_shape = (SAMPLES, SEQ, QKV)
    noise_key = jax.random.fold_in(key, stream)
    jitter = jax.random.normal(jax.random.fold_in(noise_key, 1), field_shape, jnp.float32)
    row_top = math.log(10.0)
    row_scale = jnp.exp(jax.random.uniform(jax.random.fold_in(noise_key, 3), (SAMPLES, SEQ, 1), jnp.float32, 0.0, row_top))
    col_scale = jnp.exp(jax.random.uniform(jax.random.fold_in(noise_key, 4), (1, 1, QKV), jnp.float32, 0.0, math.log(10.0)))
    return jitter * row_scale * col_scale


def draw_queries(key, part):
    field = field_draw(key, 1)
    return jnp.clip(field, -1000.0, 1000.0).astype(jnp.bfloat16)


def draw_keys(key, part):
    field = field_draw(key, 2)
    return jnp.clip(field, -1000.0, 1000.0).astype(jnp.bfloat16)


def draw_tile_lists(key, part):
    tile_count = FRAMES * TPF
    labels = jnp.arange(tile_count, dtype=jnp.int32)
    frame_of = labels // TPF
    row_of = labels % TPF // GRID_W
    col_of = labels % GRID_W
    steps_drawn = jax.random.randint(key, (SAMPLES, tile_count, KT - 1, 3), -1, 2, dtype=jnp.int32)
    frame_to = jnp.clip(frame_of[None, :, None] + steps_drawn[..., 0], 0, FRAMES - 1)
    row_to = jnp.clip(row_of[None, :, None] + steps_drawn[..., 1], 0, GRID_H - 1)
    col_to = jnp.clip(col_of[None, :, None] + steps_drawn[..., 2], 0, GRID_W - 1)
    others = frame_to * TPF + row_to * GRID_W + col_to
    itself = jnp.broadcast_to(labels[None, :, None], (SAMPLES, tile_count, 1))
    return jnp.concatenate([itself, others], axis=2).astype(jnp.int32)


def block_levels(stream_key, shape, pieces, low, top_value):
    gain, own = 1.0, jax.random.fold_in(stream_key, 6)
    for dim, shards_of in pieces:
        heights = jnp.exp(jax.random.uniform(jax.random.fold_in(own, dim), (shards_of,), jnp.float32, low / len(pieces), top_value / len(pieces)))
        gain = gain * jnp.repeat(heights, shape[dim] // shards_of).reshape([-1 if axis == dim else 1 for axis in range(len(shape))])
    return gain


def bell_draw(stream_key, shape, scale, bound, split=(), kind=jnp.bfloat16):
    drawn = jax.random.normal(stream_key, shape, jnp.float32) * scale
    if len(split) > 0:
        drawn = block_levels(stream_key, shape, split, -0.22, 0.18) * drawn
    return jnp.clip(drawn, min=-bound, max=bound).astype(kind)


def setup_inputs(seed: int = 0) -> dict:
    key_of = jax.random.split(jax.random.key(seed), 8)
    queries = draw_queries(jax.random.fold_in(key_of[7], 71), 0)
    keys = draw_keys(jax.random.fold_in(key_of[7], 71), 0)
    values = bell_draw(key_of[2], (SAMPLES, SEQ, QKV), 4.0, 24.0, ((0, 4), (1, 8)))
    targets = bell_draw(key_of[3], (SAMPLES, SEQ, QKV), 0.4, 2.390625, ((0, 4), (1, 8)))
    tile_lists = draw_tile_lists(jax.random.fold_in(key_of[7], 71), 0)
    query_gain = jnp.clip(1.0 + 0.18 * jax.random.normal(key_of[5], (QKV,), jnp.float32), 0.1, 1.9)
    key_gain = jnp.clip(1.0 + 0.18 * jax.random.normal(key_of[6], (QKV,), jnp.float32), 0.1, 1.9)
    return dict(queries=queries, keys=keys, values=values, targets=targets, tile_lists=tile_lists, query_gain=query_gain, key_gain=key_gain)


EPS = 1e-06

def norm_forward(matrix, scaling):
    widened = matrix.astype(jnp.float32)
    spread = jnp.sqrt(lax.optimization_barrier(jnp.mean(widened * widened, axis=-1, keepdims=True)) + EPS)
    unit_rows = widened / spread
    normed = lax.optimization_barrier((unit_rows * scaling).astype(jnp.bfloat16))
    return (normed, unit_rows, spread)

def norm_backward(returned, unit_rows, spread, scaling):
    upstream = returned.astype(jnp.float32) * scaling
    projected = lax.optimization_barrier(jnp.mean(upstream * unit_rows, axis=-1, keepdims=True))
    grad_matrix = ((upstream - unit_rows * projected) / spread).astype(jnp.bfloat16)
    grad_scaling = lax.optimization_barrier(jnp.sum(returned.astype(jnp.float32) * unit_rows, axis=0))
    return (grad_matrix, grad_scaling)

def window_ids(frame_index, frame_count, per_frame):
    slots = jnp.arange(3 * per_frame, dtype=jnp.int32)
    source = frame_index[:, None] + slots[None, :] // per_frame - 1
    labels = source * per_frame + slots[None, :] % per_frame
    return jnp.where((source >= 0) & (source < frame_count), labels, -1).astype(jnp.int32)

def band_mask(tile_table, labels, tile_len):
    matched = jnp.any(tile_table[:, :, :, None] == labels[:, None, None, :], axis=2)
    blocks, query_tiles, key_tiles = matched.shape
    widened = jnp.broadcast_to(matched[:, :, None, :, None], (blocks, query_tiles, tile_len, key_tiles, tile_len))
    return widened.reshape(blocks, query_tiles * tile_len, key_tiles * tile_len)

def attend(query_norm, key_window, value_window, allowed, target_block):
    factor = 1.0 / math.sqrt(query_norm.shape[-1])
    query_wide = query_norm.astype(jnp.float32)
    key_wide = key_window.astype(jnp.float32)
    value_wide = value_window.astype(jnp.float32)
    scores = jnp.einsum('bqhd,bkhd->bhqk', query_wide, key_wide) * factor
    masked = jnp.where(allowed[:, None], scores, -jnp.inf)
    highest = lax.optimization_barrier(jnp.max(masked, axis=-1, keepdims=True))
    weights = jnp.exp(masked - highest)
    shares = weights / lax.optimization_barrier(jnp.sum(weights, axis=-1, keepdims=True))
    shares_low = lax.optimization_barrier(shares.astype(jnp.bfloat16)).astype(jnp.float32)
    attended = jnp.einsum('bhqk,bkhd->bqhd', shares_low, value_wide)
    residual_out = attended - target_block.astype(jnp.float32)
    residual_low = lax.optimization_barrier(residual_out.astype(jnp.bfloat16)).astype(jnp.float32)
    value_back = jnp.einsum('bhqk,bqhd->bkhd', shares_low, residual_low)
    dshares = jnp.einsum('bqhd,bkhd->bhqk', residual_low, value_wide)
    delta = jnp.transpose(lax.optimization_barrier(jnp.sum(residual_low * attended, axis=-1)), (0, 2, 1))[..., None]
    dscores = shares * (dshares - delta) * factor
    dscores_low = lax.optimization_barrier(dscores.astype(jnp.bfloat16)).astype(jnp.float32)
    query_back = jnp.einsum('bhqk,bkhd->bqhd', dscores_low, key_wide)
    key_back = jnp.einsum('bhqk,bqhd->bkhd', dscores_low, query_wide)
    return (query_back, key_back, value_back)

def reference(queries, keys, values, targets, tile_lists, query_gain, key_gain):

    def one_sample(packed):
        sample_queries, sample_keys, sample_values, sample_targets, sample_lists = packed
        query_norm, query_unit, query_rms = norm_forward(sample_queries, query_gain)
        key_norm, key_unit, key_rms = norm_forward(sample_keys, key_gain)
        shaped = (FRAMES, FT, HEADS, HD)
        border = jnp.zeros((1, FT, HEADS, HD), jnp.bfloat16)
        query_frames = query_norm.reshape(shaped)
        key_padded = jnp.concatenate([border, key_norm.reshape(shaped), border])
        value_padded = jnp.concatenate([border, sample_values.reshape(shaped), border])
        target_frames = sample_targets.reshape(shaped)
        tile_table = sample_lists.reshape(FRAMES, TPF, KT)
        root = jnp.zeros((), jnp.int32)

        def frame_step(running, frame_at):
            key_sums, value_sums = running
            corner = (frame_at, root, root, root)
            key_window = lax.dynamic_slice(key_padded, corner, (3, FT, HEADS, HD)).reshape(1, 3 * FT, HEADS, HD)
            value_window = lax.dynamic_slice(value_padded, corner, (3, FT, HEADS, HD)).reshape(1, 3 * FT, HEADS, HD)
            labels = window_ids(jnp.reshape(frame_at, (1,)), FRAMES, TPF)
            allowed = band_mask(lax.dynamic_slice_in_dim(tile_table, frame_at, 1, 0), labels, TILE)
            query_back, key_back, value_back = attend(lax.dynamic_slice_in_dim(query_frames, frame_at, 1, 0), key_window, value_window, allowed, lax.dynamic_slice_in_dim(target_frames, frame_at, 1, 0))
            key_terms = lax.optimization_barrier(key_back.astype(jnp.bfloat16)).astype(jnp.float32)
            value_terms = lax.optimization_barrier(value_back.astype(jnp.bfloat16)).astype(jnp.float32)
            key_sums = lax.dynamic_update_slice(key_sums, lax.dynamic_slice(key_sums, corner, (3, FT, HEADS, HD)) + key_terms.reshape(3, FT, HEADS, HD), corner)
            value_sums = lax.dynamic_update_slice(value_sums, lax.dynamic_slice(value_sums, corner, (3, FT, HEADS, HD)) + value_terms.reshape(3, FT, HEADS, HD), corner)
            return ((key_sums, value_sums), query_back[0])
        zero_sums = jnp.zeros((FRAMES + 2, FT, HEADS, HD), jnp.float32)
        (key_sums, value_sums), query_back = lax.scan(frame_step, (zero_sums, zero_sums), jnp.arange(FRAMES, dtype=jnp.int32))
        query_low = query_back.reshape(SEQ, QKV).astype(jnp.bfloat16)
        key_low = key_sums[1:-1].reshape(SEQ, QKV).astype(jnp.bfloat16)
        value_low = value_sums[1:-1].reshape(SEQ, QKV).astype(jnp.bfloat16)
        grad_query_rows, query_gain_part = norm_backward(query_low, query_unit, query_rms, query_gain)
        grad_key_rows, key_gain_part = norm_backward(key_low, key_unit, key_rms, key_gain)
        return (grad_query_rows, grad_key_rows, value_low, query_gain_part, key_gain_part)
    results = lax.map(one_sample, (queries, keys, values, targets, tile_lists))
    return (results[0], results[1], results[2], lax.optimization_barrier(jnp.sum(results[3], axis=0)), lax.optimization_barrier(jnp.sum(results[4], axis=0)))
```

```python
import functools
import math

import jax
import jax.numpy as jnp
from jax import lax
from jax.experimental import pallas as pl
from jax.experimental.pallas import tpu as pltpu
from jax.sharding import PartitionSpec as P

HD = 128
TILE = 16
EPS = 1e-06
CHUNKS = 2
STEP_HEADS = 4


def norm_forward(matrix, scaling):
    widened = matrix.astype(jnp.float32)
    spread = jnp.sqrt(jnp.mean(widened * widened, axis=-1, keepdims=True) + EPS)
    return (widened / spread * scaling).astype(jnp.bfloat16), spread


def norm_backward(returned, matrix, spread, scaling):
    unit_rows = matrix.astype(jnp.float32) / spread
    upstream = returned * scaling
    projected = jnp.mean(upstream * unit_rows, axis=-1, keepdims=True)
    grad_matrix = ((upstream - unit_rows * projected) / spread).astype(jnp.bfloat16)
    return grad_matrix, jnp.sum(returned * unit_rows, axis=0)


def contract(a, b, dim_a, dim_b):
    return lax.dot_general(
        a, b, (((dim_a,), (dim_b,)), ((), ())), preferred_element_type=jnp.float32
    )


def attend_kernel(
    bias, q, kl, ko, kr, vl, vo, vr, t, dq, dkl, dko, dkr, dvl, dvo, dvr
):
    rows = q.shape[0]
    factor = 1.0 / math.sqrt(HD)
    for h in range(q.shape[1] // HD):
        at = slice(h * HD, (h + 1) * HD)
        query = q[:, at]
        key = jnp.concatenate([kl[:, at], ko[:, at], kr[:, at]], axis=0)
        value = jnp.concatenate([vl[:, at], vo[:, at], vr[:, at]], axis=0)
        scores = contract(key, query, 1, 1) * factor + bias[...]
        weights = jnp.exp(scores - jnp.max(scores, axis=0, keepdims=True))
        shares = weights * (1.0 / jnp.sum(weights, axis=0, keepdims=True))
        shares_low = shares.astype(jnp.bfloat16)
        attended = contract(value, shares_low, 0, 0)
        wanted = t[:, at].astype(jnp.float32).T
        residual_low = (attended - wanted).astype(jnp.bfloat16)
        residual_wide = residual_low.astype(jnp.float32)
        delta = jnp.sum(residual_wide * attended, axis=0, keepdims=True)
        dvalue = contract(shares_low, residual_low, 1, 1).astype(jnp.bfloat16)
        dshares = contract(value, residual_low, 1, 0)
        dscores_low = (shares * (dshares - delta) * factor).astype(jnp.bfloat16)
        dkey = contract(dscores_low, query, 1, 0).astype(jnp.bfloat16)
        dq[:, at] = contract(key, dscores_low, 0, 0).T.astype(jnp.bfloat16)
        dkl[:, at], dko[:, at], dkr[:, at] = (
            dkey[:rows],
            dkey[rows : 2 * rows],
            dkey[2 * rows :],
        )
        dvl[:, at], dvo[:, at], dvr[:, at] = (
            dvalue[:rows],
            dvalue[rows : 2 * rows],
            dvalue[2 * rows :],
        )


def attend(chunk, width, bias, q, kl, ko, kr, vl, vo, vr, t):
    rows = q.shape[0]
    block = min(STEP_HEADS * HD, width)
    steps = width // block
    heads = width // HD
    whole = pl.BlockSpec((rows, block), lambda i: (0, chunk * steps + i))
    part = pl.BlockSpec((rows, block), lambda i: (0, i))
    fixed = pl.BlockSpec(bias.shape, lambda i: (0, 0))
    out = jax.ShapeDtypeStruct((rows, width), jnp.bfloat16)
    return pl.pallas_call(
        attend_kernel,
        grid=(steps,),
        in_specs=[fixed, whole, part, whole, part, part, whole, part, whole],
        out_specs=[part] * 7,
        out_shape=[out] * 7,
        cost_estimate=pl.CostEstimate(
            flops=5 * 2 * rows * 3 * rows * HD * heads * 3,
            bytes_accessed=15 * rows * width * 2,
            transcendentals=3 * rows * rows * heads,
        ),
    )(bias, q, kl, ko, kr, vl, vo, vr, t)


def shards(queries, keys, values, targets, tile_lists, query_gain, key_gain):
    q, k, v, t = queries[0], keys[0], values[0], targets[0]
    rows, features = q.shape
    frame_count = lax.axis_size("seq")
    frame = lax.axis_index("seq")
    rightward = [(i, i + 1) for i in range(frame_count - 1)]
    leftward = [(i + 1, i) for i in range(frame_count - 1)]
    to_right = lambda x: lax.ppermute(x, "seq", rightward)
    to_left = lambda x: lax.ppermute(x, "seq", leftward)

    gains = lax.all_gather(jnp.stack([query_gain, key_gain]), "fsdp", axis=1, tiled=True)
    query_scale, key_scale = gains[0], gains[1]
    key_norm, key_rms = norm_forward(k, key_scale)
    query_norm, query_rms = norm_forward(q, query_scale)

    tiles = rows // TILE
    lists = jnp.repeat(tile_lists[0], TILE, axis=0).T
    labels = (frame - 1) * tiles + jnp.arange(3 * rows, dtype=jnp.int32) // TILE
    labels = jnp.where((labels >= 0) & (labels < frame_count * tiles), labels, -1)[:, None]
    allowed = lists[0:1] == labels
    for slot in range(1, lists.shape[0]):
        allowed = allowed | (lists[slot : slot + 1] == labels)
    bias = jnp.where(allowed, 0.0, -jnp.inf).astype(jnp.float32)

    width = features // CHUNKS
    held = []
    before = None
    for c in range(CHUNKS):
        at = slice(c * width, (c + 1) * width)
        v_part, k_part = v[:, at], key_norm[:, at]
        if before is not None:
            v_part, _ = lax.optimization_barrier((v_part, before[0]))
            k_part, _ = lax.optimization_barrier((k_part, before[1]))
        vl, vr = to_right(v_part), to_left(v_part)
        kl, kr = to_right(k_part), to_left(k_part)
        before = (vl, kl)
        held.append((kl, kr, vl, vr))

    dq, dk, dv = [], [], []
    for c in range(CHUNKS):
        kl, kr, vl, vr = held[c]
        dq_c, dkl, dko, dkr, dvl, dvo, dvr = attend(
            c, width, bias, query_norm, kl, key_norm, kr, vl, v, vr, t
        )
        dq.append(dq_c.astype(jnp.float32))
        wide = lambda a, b, d: sum(x.astype(jnp.float32) for x in (a, b, d))
        dk.append(wide(dko, to_left(dkl), to_right(dkr)).astype(jnp.bfloat16).astype(jnp.float32))
        dv.append(wide(dvo, to_left(dvl), to_right(dvr)).astype(jnp.bfloat16))

    grad_q, q_gain = norm_backward(jnp.concatenate(dq, axis=1), q, query_rms, query_scale)
    grad_k, k_gain = norm_backward(jnp.concatenate(dk, axis=1), k, key_rms, key_scale)
    span = query_gain.shape[0]
    own = lax.axis_index("fsdp") * span
    gain_grads = [
        lax.dynamic_slice_in_dim(lax.psum(x, ("seq", "fsdp")), own, span) for x in (q_gain, k_gain)
    ]
    return (
        grad_q[None],
        grad_k[None],
        jnp.concatenate(dv, axis=1)[None],
        gain_grads[0],
        gain_grads[1],
    )


def solution(mesh):
    rows = P("fsdp", "seq", None)
    return jax.shard_map(
        shards,
        mesh=mesh,
        in_specs=(rows, rows, rows, rows, rows, P("fsdp"), P("fsdp")),
        out_specs=(rows, rows, rows, P("fsdp"), P("fsdp")),
        check_vma=False,
    )
```

```python
import functools
import math

import jax
import jax.numpy as jnp
from jax import lax
from jax.experimental import pallas as pl
from jax.experimental.pallas import tpu as pltpu
from jax.sharding import PartitionSpec as P

HD = 128
TILE = 16
EPS = 1e-06
CHUNKS = 2
STEP_HEADS = 4


def norm_forward(matrix, scaling):
    widened = matrix.astype(jnp.float32)
    spread = jnp.sqrt(jnp.mean(widened * widened, axis=-1, keepdims=True) + EPS)
    return (widened / spread * scaling).astype(jnp.bfloat16), spread


def norm_backward(returned, matrix, spread, scaling):
    unit_rows = matrix.astype(jnp.float32) / spread
    upstream = returned * scaling
    projected = jnp.mean(upstream * unit_rows, axis=-1, keepdims=True)
    grad_matrix = ((upstream - unit_rows * projected) / spread).astype(jnp.bfloat16)
    return grad_matrix, jnp.sum(returned * unit_rows, axis=0)


def contract(a, b, dim_a, dim_b):
    return lax.dot_general(
        a, b, (((dim_a,), (dim_b,)), ((), ())), preferred_element_type=jnp.float32
    )


def attend_kernel(
    bias, q, kl, ko, kr, vl, vo, vr, t, dq, dkl, dko, dkr, dvl, dvo, dvr
):
    rows = q.shape[0]
    factor = 1.0 / math.sqrt(HD)
    for h in range(q.shape[1] // HD):
        at = slice(h * HD, (h + 1) * HD)
        query = q[:, at]
        key = jnp.concatenate([kl[:, at], ko[:, at], kr[:, at]], axis=0)
        value = jnp.concatenate([vl[:, at], vo[:, at], vr[:, at]], axis=0)
        scores = contract(key, query, 1, 1) * factor + bias[...]
        weights = jnp.exp(scores - jnp.max(scores, axis=0, keepdims=True))
        shares = weights * (1.0 / jnp.sum(weights, axis=0, keepdims=True))
        shares_low = shares.astype(jnp.bfloat16)
        attended = contract(value, shares_low, 0, 0)
        wanted = t[:, at].astype(jnp.float32).T
        residual_low = (attended - wanted).astype(jnp.bfloat16)
        residual_wide = residual_low.astype(jnp.float32)
        delta = jnp.sum(residual_wide * attended, axis=0, keepdims=True)
        dvalue = contract(shares_low, residual_low, 1, 1).astype(jnp.bfloat16)
        dshares = contract(value, residual_low, 1, 0)
        dscores_low = (shares * (dshares - delta) * factor).astype(jnp.bfloat16)
        dkey = contract(dscores_low, query, 1, 0).astype(jnp.bfloat16)
        dq[:, at] = contract(key, dscores_low, 0, 0).T.astype(jnp.bfloat16)
        dkl[:, at], dko[:, at], dkr[:, at] = (
            dkey[:rows],
            dkey[rows : 2 * rows],
            dkey[2 * rows :],
        )
        dvl[:, at], dvo[:, at], dvr[:, at] = (
            dvalue[:rows],
            dvalue[rows : 2 * rows],
            dvalue[2 * rows :],
        )


def attend(chunk, width, bias, q, kl, ko, kr, vl, vo, vr, t):
    rows = q.shape[0]
    block = min(STEP_HEADS * HD, width)
    steps = width // block
    heads = width // HD
    whole = pl.BlockSpec((rows, block), lambda i: (0, chunk * steps + i))
    part = pl.BlockSpec((rows, block), lambda i: (0, i))
    fixed = pl.BlockSpec(bias.shape, lambda i: (0, 0))
    out = jax.ShapeDtypeStruct((rows, width), jnp.bfloat16)
    return pl.pallas_call(
        attend_kernel,
        grid=(steps,),
        in_specs=[fixed, whole, part, whole, part, part, whole, part, whole],
        out_specs=[part] * 7,
        out_shape=[out] * 7,
        cost_estimate=pl.CostEstimate(
            flops=5 * 2 * rows * 3 * rows * HD * heads * 3,
            bytes_accessed=15 * rows * width * 2,
            transcendentals=3 * rows * rows * heads,
        ),
    )(bias, q, kl, ko, kr, vl, vo, vr, t)


def gather_gains(part):
    count, me = lax.axis_size("fsdp"), lax.axis_index("fsdp")
    pieces = [part] + [
        lax.ppermute(part, "fsdp", [(i, (i + s) % count) for i in range(count)])
        for s in range(1, count)
    ]
    blocks = []
    for j in range(count):
        block = pieces[0]
        for s in range(1, count):
            block = jnp.where((me - s - j) % count == 0, pieces[s], block)
        blocks.append(block)
    return jnp.concatenate(blocks, axis=1)


def sum_gains(parts):
    count, me = lax.axis_size("fsdp"), lax.axis_index("fsdp")
    blocks = parts.reshape(parts.shape[0], count, -1)
    total = lax.dynamic_index_in_dim(blocks, me, axis=1, keepdims=False)
    for s in range(1, count):
        there = lax.dynamic_index_in_dim(blocks, (me + s) % count, axis=1, keepdims=False)
        total = total + lax.ppermute(there, "fsdp", [(i, (i + s) % count) for i in range(count)])
    frame_count = lax.axis_size("seq")
    if frame_count & (frame_count - 1):
        return lax.psum(total, "seq")
    step = 1
    while step < frame_count:
        total = total + lax.ppermute(total, "seq", [(i, i ^ step) for i in range(frame_count)])
        step *= 2
    return total


def shards(queries, keys, values, targets, tile_lists, query_gain, key_gain):
    q, k, v, t = queries[0], keys[0], values[0], targets[0]
    rows, features = q.shape
    frame_count = lax.axis_size("seq")
    frame = lax.axis_index("seq")
    rightward = [(i, i + 1) for i in range(frame_count - 1)]
    leftward = [(i + 1, i) for i in range(frame_count - 1)]
    to_right = lambda x: lax.ppermute(x, "seq", rightward)
    to_left = lambda x: lax.ppermute(x, "seq", leftward)

    middle = frame_count // 2
    near = lambda pairs: [p for p in pairs if set(p) != {middle - 1, middle}]
    near_right = lambda x: lax.ppermute(x, "seq", near(rightward))
    near_left = lambda x: lax.ppermute(x, "seq", near(leftward))

    def relay(x):
        out = lax.ppermute(x, "seq", [(middle - 1, frame_count - 1), (middle, 0)])
        return lax.ppermute(out, "seq", [(frame_count - 1, middle), (0, middle - 1)])

    gains = gather_gains(jnp.stack([query_gain, key_gain]))
    query_scale, key_scale = gains[0], gains[1]
    key_norm, key_rms = norm_forward(k, key_scale)
    query_norm, query_rms = norm_forward(q, query_scale)

    tiles = rows // TILE
    lists = jnp.repeat(tile_lists[0], TILE, axis=0).T
    labels = (frame - 1) * tiles + jnp.arange(3 * rows, dtype=jnp.int32) // TILE
    labels = jnp.where((labels >= 0) & (labels < frame_count * tiles), labels, -1)[:, None]
    allowed = lists[0:1] == labels
    for slot in range(1, lists.shape[0]):
        allowed = allowed | (lists[slot : slot + 1] == labels)
    bias = jnp.where(allowed, 0.0, -jnp.inf).astype(jnp.float32)

    width = features // CHUNKS
    held = []
    before = None
    for c in range(CHUNKS):
        at = slice(c * width, (c + 1) * width)
        v_part, k_part = v[:, at], key_norm[:, at]
        if before is not None:
            v_part, _ = lax.optimization_barrier((v_part, before[0]))
            k_part, _ = lax.optimization_barrier((k_part, before[1]))
        vl, vr = to_right(v_part), to_left(v_part)
        far = relay(k_part)
        kl, kr = near_right(k_part), near_left(k_part)
        before = (vl, kl)
        kl, kr = jnp.where(frame == middle, far, kl), jnp.where(frame == middle - 1, far, kr)
        held.append((kl, kr, vl, vr))

    dq, dk, dv = [], [], []
    for c in range(CHUNKS):
        kl, kr, vl, vr = held[c]
        dq_c, dkl, dko, dkr, dvl, dvo, dvr = attend(
            c, width, bias, query_norm, kl, key_norm, kr, vl, v, vr, t
        )
        dq.append(dq_c.astype(jnp.float32))
        wide = lambda *terms: sum(x.astype(jnp.float32) for x in terms)
        dk.append(wide(dko, to_left(dkl), to_right(dkr)).astype(jnp.bfloat16).astype(jnp.float32))
        far = relay(jnp.where(frame == middle, dvl, dvr))
        dv.append(wide(dvo, near_left(dvl), near_right(dvr), far).astype(jnp.bfloat16))

    grad_q, q_gain = norm_backward(jnp.concatenate(dq, axis=1), q, query_rms, query_scale)
    grad_k, k_gain = norm_backward(jnp.concatenate(dk, axis=1), k, key_rms, key_scale)
    gain_grads = sum_gains(jnp.stack([q_gain, k_gain]))
    return (
        grad_q[None],
        grad_k[None],
        jnp.concatenate(dv, axis=1)[None],
        gain_grads[0],
        gain_grads[1],
    )


def solution(mesh):
    rows = P("fsdp", "seq", None)
    return jax.shard_map(
        shards,
        mesh=mesh,
        in_specs=(rows, rows, rows, rows, rows, P("fsdp"), P("fsdp")),
        out_specs=(rows, rows, rows, P("fsdp"), P("fsdp")),
        check_vma=False,
    )
```

```python
import math

import jax
import jax.numpy as jnp
from jax import lax
from jax.experimental import pallas as pl
from jax.sharding import PartitionSpec as P


HD = 128
TILE = 16
EPS = 1e-06
CHUNKS = 2
STEP_HEADS = 4


def norm_forward(matrix, scaling):
    widened = matrix.astype(jnp.float32)
    spread = jnp.sqrt(jnp.mean(widened * widened, axis=-1, keepdims=True) + EPS)
    return (widened / spread * scaling).astype(jnp.bfloat16), spread


def norm_backward(returned, matrix, spread, scaling):
    unit_rows = matrix.astype(jnp.float32) / spread
    upstream = returned * scaling
    projected = jnp.mean(upstream * unit_rows, axis=-1, keepdims=True)
    grad_matrix = ((upstream - unit_rows * projected) / spread).astype(jnp.bfloat16)
    return grad_matrix, jnp.sum(returned * unit_rows, axis=0)


def contract(a, b, dim_a, dim_b):
    return lax.dot_general(
        a, b, (((dim_a,), (dim_b,)), ((), ())), preferred_element_type=jnp.float32
    )


def attend_kernel(
    bias, q, kl, ko, kr, vl, vo, vr, t, dq, dkl, dko, dkr, dvl, dvo, dvr
):
    rows = q.shape[0]
    factor = 1.0 / math.sqrt(HD)
    for h in range(q.shape[1] // HD):
        at = slice(h * HD, (h + 1) * HD)
        query = q[:, at]
        key = jnp.concatenate([kl[:, at], ko[:, at], kr[:, at]], axis=0)
        value = jnp.concatenate([vl[:, at], vo[:, at], vr[:, at]], axis=0)
        scores = contract(key, query, 1, 1) * factor + bias[...]
        weights = jnp.exp(scores - jnp.max(scores, axis=0, keepdims=True))
        shares = weights * (1.0 / jnp.sum(weights, axis=0, keepdims=True))
        shares_low = shares.astype(jnp.bfloat16)
        attended = contract(value, shares_low, 0, 0)
        wanted = t[:, at].astype(jnp.float32).T
        residual_low = (attended - wanted).astype(jnp.bfloat16)
        residual_wide = residual_low.astype(jnp.float32)
        delta = jnp.sum(residual_wide * attended, axis=0, keepdims=True)
        dvalue = contract(shares_low, residual_low, 1, 1).astype(jnp.bfloat16)
        dshares = contract(value, residual_low, 1, 0)
        dscores_low = (shares * (dshares - delta) * factor).astype(jnp.bfloat16)
        dkey = contract(dscores_low, query, 1, 0).astype(jnp.bfloat16)
        dq[:, at] = contract(key, dscores_low, 0, 0).T.astype(jnp.bfloat16)
        dkl[:, at], dko[:, at], dkr[:, at] = (
            dkey[:rows],
            dkey[rows : 2 * rows],
            dkey[2 * rows :],
        )
        dvl[:, at], dvo[:, at], dvr[:, at] = (
            dvalue[:rows],
            dvalue[rows : 2 * rows],
            dvalue[2 * rows :],
        )


def attend(chunk, width, bias, q, kl, ko, kr, vl, vo, vr, t):
    rows = q.shape[0]
    block = min(STEP_HEADS * HD, width)
    steps = width // block
    heads = width // HD
    whole = pl.BlockSpec((rows, block), lambda i: (0, chunk * steps + i))
    part = pl.BlockSpec((rows, block), lambda i: (0, i))
    fixed = pl.BlockSpec(bias.shape, lambda i: (0, 0))
    out = jax.ShapeDtypeStruct((rows, width), jnp.bfloat16)
    return pl.pallas_call(
        attend_kernel,
        grid=(steps,),
        in_specs=[fixed, whole, part, whole, part, part, whole, part, whole],
        out_specs=[part] * 7,
        out_shape=[out] * 7,
        cost_estimate=pl.CostEstimate(
            flops=5 * 2 * rows * 3 * rows * HD * heads * 3,
            bytes_accessed=15 * rows * width * 2,
            transcendentals=3 * rows * rows * heads,
        ),
    )(bias, q, kl, ko, kr, vl, vo, vr, t)


def gather_gains(part):
    count, me = lax.axis_size("fsdp"), lax.axis_index("fsdp")
    pieces = [part] + [
        lax.ppermute(part, "fsdp", [(i, (i + s) % count) for i in range(count)])
        for s in range(1, count)
    ]
    blocks = []
    for j in range(count):
        block = pieces[0]
        for s in range(1, count):
            block = jnp.where((me - s - j) % count == 0, pieces[s], block)
        blocks.append(block)
    return jnp.concatenate(blocks, axis=1)


def sum_gains(parts):
    count, me = lax.axis_size("fsdp"), lax.axis_index("fsdp")
    blocks = parts.reshape(parts.shape[0], count, -1)
    total = lax.dynamic_index_in_dim(blocks, me, axis=1, keepdims=False)
    for s in range(1, count):
        there = lax.dynamic_index_in_dim(blocks, (me + s) % count, axis=1, keepdims=False)
        total = total + lax.ppermute(there, "fsdp", [(i, (i + s) % count) for i in range(count)])
    frame_count = lax.axis_size("seq")
    if frame_count & (frame_count - 1):
        return lax.psum(total, "seq")
    step = 1
    while step < frame_count:
        total = total + lax.ppermute(total, "seq", [(i, i ^ step) for i in range(frame_count)])
        step *= 2
    return total


def shards(queries, keys, values, targets, tile_lists, query_gain, key_gain):
    q, k, v, t = queries[0], keys[0], values[0], targets[0]
    rows, features = q.shape
    frame_count = lax.axis_size("seq")
    frame = lax.axis_index("seq")
    rightward = [(i, i + 1) for i in range(frame_count - 1)]
    leftward = [(i + 1, i) for i in range(frame_count - 1)]
    to_right = lambda x: lax.ppermute(x, "seq", rightward)
    to_left = lambda x: lax.ppermute(x, "seq", leftward)

    middle = frame_count // 2
    near = lambda pairs: [p for p in pairs if set(p) != {middle - 1, middle}]
    near_right = lambda x: lax.ppermute(x, "seq", near(rightward))
    near_left = lambda x: lax.ppermute(x, "seq", near(leftward))

    def relay(x):
        out = lax.ppermute(x, "seq", [(middle - 1, frame_count - 1), (middle, 0)])
        return lax.ppermute(out, "seq", [(frame_count - 1, middle), (0, middle - 1)])

    v_far = relay(v)
    gains = gather_gains(jnp.stack([query_gain, key_gain]))
    query_scale, key_scale = gains[0], gains[1]
    key_norm, key_rms = norm_forward(k, key_scale)
    query_norm, query_rms = norm_forward(q, query_scale)

    tiles = rows // TILE
    lists = jnp.repeat(tile_lists[0], TILE, axis=0).T
    labels = (frame - 1) * tiles + jnp.arange(3 * rows, dtype=jnp.int32) // TILE
    labels = jnp.where((labels >= 0) & (labels < frame_count * tiles), labels, -1)[:, None]
    allowed = lists[0:1] == labels
    for slot in range(1, lists.shape[0]):
        allowed = allowed | (lists[slot : slot + 1] == labels)
    bias = jnp.where(allowed, 0.0, -jnp.inf).astype(jnp.float32)

    width = features // CHUNKS
    held = []
    before = None
    for c in range(CHUNKS):
        at = slice(c * width, (c + 1) * width)
        v_part, k_part = v[:, at], key_norm[:, at]
        if before is not None:
            v_part, _ = lax.optimization_barrier((v_part, before[0]))
            k_part, _ = lax.optimization_barrier((k_part, before[1]))
        vl, vr = near_right(v_part), near_left(v_part)
        kl, kr = to_right(k_part), to_left(k_part)
        before = (vl, kl)
        held.append((kl, kr, vl, vr))

    dq, dk, dv = [], [], []
    for c in range(CHUNKS):
        kl, kr, vl, vr = held[c]
        far = v_far
        if c > 0:
            vl, vr, far, _ = lax.optimization_barrier((vl, vr, v_far, dq_c))
        far = far[:, c * width : (c + 1) * width]
        vl = jnp.where(frame == middle, far, vl)
        vr = jnp.where(frame == middle - 1, far, vr)
        dq_c, dkl, dko, dkr, dvl, dvo, dvr = attend(
            c, width, bias, query_norm, kl, key_norm, kr, vl, v, vr, t
        )
        dq.append(dq_c.astype(jnp.float32))
        if c == 0:
            far = relay(
                jnp.concatenate(
                    [jnp.where(frame == middle, dkl, dkr), jnp.where(frame == middle, dvl, dvr)]
                ),
            )
            k_terms = (dko, near_left(dkl), near_right(dkr), far[:rows])
            v_terms = (dvo, near_left(dvl), near_right(dvr), far[rows:])
        else:
            k_terms = (dko, to_left(dkl), to_right(dkr))
            v_terms = (dvo, to_left(dvl), to_right(dvr))
        wide = lambda terms: sum(x.astype(jnp.float32) for x in terms).astype(jnp.bfloat16)
        dk.append(wide(k_terms).astype(jnp.float32))
        dv.append(wide(v_terms))

    grad_q, q_gain = norm_backward(jnp.concatenate(dq, axis=1), q, query_rms, query_scale)
    grad_k, k_gain = norm_backward(jnp.concatenate(dk, axis=1), k, key_rms, key_scale)
    gain_grads = sum_gains(jnp.stack([q_gain, k_gain]))
    return (
        grad_q[None],
        grad_k[None],
        jnp.concatenate(dv, axis=1)[None],
        gain_grads[0],
        gain_grads[1],
    )


def solution(mesh):
    rows = P("fsdp", "seq", None)
    return jax.shard_map(
        shards,
        mesh=mesh,
        in_specs=(rows, rows, rows, rows, rows, P("fsdp"), P("fsdp")),
        out_specs=(rows, rows, rows, P("fsdp"), P("fsdp")),
        check_vma=False,
    )
```

```python
import math

import jax
import jax.numpy as jnp
from jax import lax
from jax.experimental import pallas as pl
from jax.sharding import PartitionSpec as P


HD = 128
TILE = 16
EPS = 1e-06
CHUNKS = 2
STEP_HEADS = 4


def norm_forward(matrix, scaling):
    widened = matrix.astype(jnp.float32)
    spread = jnp.sqrt(jnp.mean(widened * widened, axis=-1, keepdims=True) + EPS)
    return (widened / spread * scaling).astype(jnp.bfloat16), spread


def norm_backward(returned, matrix, spread, scaling):
    unit_rows = matrix.astype(jnp.float32) / spread
    upstream = returned * scaling
    projected = jnp.mean(upstream * unit_rows, axis=-1, keepdims=True)
    grad_matrix = ((upstream - unit_rows * projected) / spread).astype(jnp.bfloat16)
    return grad_matrix, jnp.sum(returned * unit_rows, axis=0)


def contract(a, b, dim_a, dim_b):
    return lax.dot_general(
        a, b, (((dim_a,), (dim_b,)), ((), ())), preferred_element_type=jnp.float32
    )


def attend_kernel(
    bias, q, kl, ko, kr, vl, vo, vr, t, dq, dkl, dko, dkr, dvl, dvo, dvr
):
    rows = q.shape[0]
    factor = 1.0 / math.sqrt(HD)
    for h in range(q.shape[1] // HD):
        at = slice(h * HD, (h + 1) * HD)
        query = q[:, at]
        key = jnp.concatenate([kl[:, at], ko[:, at], kr[:, at]], axis=0)
        value = jnp.concatenate([vl[:, at], vo[:, at], vr[:, at]], axis=0)
        scores = contract(key, query, 1, 1) * factor + bias[...]
        weights = jnp.exp(scores - jnp.max(scores, axis=0, keepdims=True))
        shares = weights * (1.0 / jnp.sum(weights, axis=0, keepdims=True))
        shares_low = shares.astype(jnp.bfloat16)
        attended = contract(value, shares_low, 0, 0)
        wanted = t[:, at].astype(jnp.float32).T
        residual_low = (attended - wanted).astype(jnp.bfloat16)
        residual_wide = residual_low.astype(jnp.float32)
        delta = jnp.sum(residual_wide * attended, axis=0, keepdims=True)
        dvalue = contract(shares_low, residual_low, 1, 1).astype(jnp.bfloat16)
        dshares = contract(value, residual_low, 1, 0)
        dscores_low = (shares * (dshares - delta) * factor).astype(jnp.bfloat16)
        dkey = contract(dscores_low, query, 1, 0).astype(jnp.bfloat16)
        dq[:, at] = contract(key, dscores_low, 0, 0).T.astype(jnp.bfloat16)
        dkl[:, at], dko[:, at], dkr[:, at] = (
            dkey[:rows],
            dkey[rows : 2 * rows],
            dkey[2 * rows :],
        )
        dvl[:, at], dvo[:, at], dvr[:, at] = (
            dvalue[:rows],
            dvalue[rows : 2 * rows],
            dvalue[2 * rows :],
        )


def attend(chunk, width, bias, q, kl, ko, kr, vl, vo, vr, t):
    rows = q.shape[0]
    block = min(STEP_HEADS * HD, width)
    steps = width // block
    heads = width // HD
    whole = pl.BlockSpec((rows, block), lambda i: (0, chunk * steps + i))
    part = pl.BlockSpec((rows, block), lambda i: (0, i))
    fixed = pl.BlockSpec(bias.shape, lambda i: (0, 0))
    out = jax.ShapeDtypeStruct((rows, width), jnp.bfloat16)
    return pl.pallas_call(
        attend_kernel,
        grid=(steps,),
        in_specs=[fixed, whole, part, whole, part, part, whole, part, whole],
        out_specs=[part] * 7,
        out_shape=[out] * 7,
        cost_estimate=pl.CostEstimate(
            flops=5 * 2 * rows * 3 * rows * HD * heads * 3,
            bytes_accessed=15 * rows * width * 2,
            transcendentals=3 * rows * rows * heads,
        ),
    )(bias, q, kl, ko, kr, vl, vo, vr, t)


def gather_gains(part):
    count, me = lax.axis_size("fsdp"), lax.axis_index("fsdp")
    pieces = [part] + [
        lax.ppermute(part, "fsdp", [(i, (i + s) % count) for i in range(count)])
        for s in range(1, count)
    ]
    blocks = []
    for j in range(count):
        block = pieces[0]
        for s in range(1, count):
            block = jnp.where((me - s - j) % count == 0, pieces[s], block)
        blocks.append(block)
    return jnp.concatenate(blocks, axis=1)


def sum_gains(parts):
    count, me = lax.axis_size("fsdp"), lax.axis_index("fsdp")
    blocks = parts.reshape(parts.shape[0], count, -1)
    total = lax.dynamic_index_in_dim(blocks, me, axis=1, keepdims=False)
    for s in range(1, count):
        there = lax.dynamic_index_in_dim(blocks, (me + s) % count, axis=1, keepdims=False)
        total = total + lax.ppermute(there, "fsdp", [(i, (i + s) % count) for i in range(count)])
    frame_count = lax.axis_size("seq")
    if frame_count & (frame_count - 1):
        return lax.psum(total, "seq")
    step = 1
    while step < frame_count:
        total = total + lax.ppermute(total, "seq", [(i, i ^ step) for i in range(frame_count)])
        step *= 2
    return total


def shards(queries, keys, values, targets, tile_lists, query_gain, key_gain):
    q, k, v, t = queries[0], keys[0], values[0], targets[0]
    rows, features = q.shape
    frame_count = lax.axis_size("seq")
    frame = lax.axis_index("seq")
    rightward = [(i, i + 1) for i in range(frame_count - 1)]
    leftward = [(i + 1, i) for i in range(frame_count - 1)]
    to_right = lambda x: lax.ppermute(x, "seq", rightward)
    to_left = lambda x: lax.ppermute(x, "seq", leftward)

    middle = frame_count // 2
    near = lambda pairs: [p for p in pairs if set(p) != {middle - 1, middle}]
    near_right = lambda x: lax.ppermute(x, "seq", near(rightward))
    near_left = lambda x: lax.ppermute(x, "seq", near(leftward))

    def relay(x):
        out = lax.ppermute(x, "seq", [(middle - 1, frame_count - 1), (middle, 0)])
        return lax.ppermute(out, "seq", [(frame_count - 1, middle), (0, middle - 1)])

    v_far = relay(v)
    gains = gather_gains(jnp.stack([query_gain, key_gain]))
    query_scale, key_scale = gains[0], gains[1]
    key_norm, key_rms = norm_forward(k, key_scale)
    query_norm, query_rms = norm_forward(q, query_scale)

    tiles = rows // TILE
    lists = jnp.repeat(tile_lists[0], TILE, axis=0).T
    labels = (frame - 1) * tiles + jnp.arange(3 * rows, dtype=jnp.int32) // TILE
    labels = jnp.where((labels >= 0) & (labels < frame_count * tiles), labels, -1)[:, None]
    allowed = lists[0:1] == labels
    for slot in range(1, lists.shape[0]):
        allowed = allowed | (lists[slot : slot + 1] == labels)
    bias = jnp.where(allowed, 0.0, -jnp.inf).astype(jnp.float32)

    width = features // CHUNKS
    held = []
    before = None
    for c in range(CHUNKS):
        at = slice(c * width, (c + 1) * width)
        v_part, k_part = v[:, at], key_norm[:, at]
        if before is not None:
            v_part, _ = lax.optimization_barrier((v_part, before[0]))
            k_part, _ = lax.optimization_barrier((k_part, before[1]))
        vl, vr = near_right(v_part), near_left(v_part)
        kl, kr = to_right(k_part), to_left(k_part)
        before = (vl, kl)
        held.append((kl, kr, vl, vr))

    dq, dk, dv = [], [], []
    for c in range(CHUNKS):
        kl, kr, vl, vr = held[c]
        far = v_far
        if c > 0:
            vl, vr, far, _ = lax.optimization_barrier((vl, vr, v_far, dq_c))
        far = far[:, c * width : (c + 1) * width]
        vl = jnp.where(frame == middle, far, vl)
        vr = jnp.where(frame == middle - 1, far, vr)
        dq_c, dkl, dko, dkr, dvl, dvo, dvr = attend(
            c, width, bias, query_norm, kl, key_norm, kr, vl, v, vr, t
        )
        dq.append(dq_c.astype(jnp.float32))
        if c == 0:
            far = relay(jnp.where(frame == middle, dvl, dvr))
            k_terms = (dko, to_left(dkl), to_right(dkr))
            v_terms = (dvo, near_left(dvl), near_right(dvr), far)
        else:
            k_from_right, k_from_left = to_left(dkl), to_right(dkr)
            k_terms = (dko, k_from_right, k_from_left)
            dvl, dvr, k_from_right, k_from_left = lax.optimization_barrier(
                (dvl, dvr, k_from_right, k_from_left)
            )
            v_terms = (dvo, to_left(dvl), to_right(dvr))
        wide = lambda terms: sum(x.astype(jnp.float32) for x in terms).astype(jnp.bfloat16)
        dk.append(wide(k_terms).astype(jnp.float32))
        dv.append(wide(v_terms))

    grad_q, q_gain = norm_backward(jnp.concatenate(dq, axis=1), q, query_rms, query_scale)
    grad_k, k_gain = norm_backward(jnp.concatenate(dk, axis=1), k, key_rms, key_scale)
    gain_grads = sum_gains(jnp.stack([q_gain, k_gain]))
    return (
        grad_q[None],
        grad_k[None],
        jnp.concatenate(dv, axis=1)[None],
        gain_grads[0],
        gain_grads[1],
    )


def solution(mesh):
    rows = P("fsdp", "seq", None)
    return jax.shard_map(
        shards,
        mesh=mesh,
        in_specs=(rows, rows, rows, rows, rows, P("fsdp"), P("fsdp")),
        out_specs=(rows, rows, rows, P("fsdp"), P("fsdp")),
        check_vma=False,
    )
```
